768 devices in a mesh: space: 24 (over x, z_lo), band: 32 (over z_hi, y, core).
Axes of the slice: x: 4, y: 8, z: 12 (z_hi: 2, z_lo: 6; z = z_hi * 6 + z_lo), core: 2. Of those that a mesh axis runs over, the one named last changes fastest.
Arguments:
- orbitals: float32 [768, 48, 2048], P('band', 'space'), may hold values from -6 to 6
- potential: float32 [48, 2048], P('space'), may hold values from 0 to 2
Outputs:
- filtered: float32 [768, 48, 2048], P('band', 'space')
- margin: float32 [768, 768], P('band')
The draws below stay inside these ranges and needn't reach their ends.
All inputs are finite; a program needn't handle non-finite values.
Results may differ from the reference program's by a relative error of at most 0.0002.
Values sent between devices are 32-bit elements; how exact they have to be, the bound alone decides.
A program may use at most 32 MiB of HBM per device.

```python
import jax
import jax.numpy as jnp
from jax import lax

ORBS = 768
NY = 32
NZ = 64
NX = 48
N_BAND = 32


def raised(array, own_key, source, target, shards_of, factor):
    owner, partner = [(jnp.arange(array.shape[position]) // (array.shape[position] // shards_of)).reshape([-1 if axis == position else 1 for axis in range(array.ndim)]) for position in (source, target)]
    chosen = jax.random.permutation(own_key, shards_of)[partner]
    strong = (owner == chosen) | (owner == (partner + shards_of // 2) % shards_of)
    return jnp.where(strong, factor * array, array)


def block_levels(rng, extent, pieces, low, largest):
    level, own = 1.0, jax.random.fold_in(rng, 6)
    for position, parts in pieces:
        steps = jnp.exp(jax.random.uniform(jax.random.fold_in(own, position), (parts,), jnp.float32, low / len(pieces), largest / len(pieces)))
        level = level * jnp.repeat(steps, extent[position] // parts).reshape([-1 if axis == position else 1 for axis in range(len(extent))])
    return level


def bell_draw_with(rng, shape, width, bound, shards, heavy, kind=jnp.bfloat16):
    drawn = width * jax.random.normal(rng, shape, jnp.float32)
    if shards:
        drawn = drawn * block_levels(rng, shape, shards, -0.22, 0.18)
    return jnp.clip(raised(drawn, jax.random.fold_in(rng, 3), *heavy), -bound, bound).astype(kind)


def setup_inputs(seed: int = 0) -> dict:
    key_of = jax.random.split(jax.random.key(seed), 3)
    return {
        "orbitals": bell_draw_with(key_of[0], (ORBS, NX, NY * NZ), 1.0, 6.0, ((0, 32), (1, 24)), (1, 0, 16, 2.0), jnp.float32),
        "potential": jnp.clip(2.0 * jax.random.uniform(key_of[1], (NX, NY * NZ), jnp.float32) ** block_levels(key_of[1], (NX, NY * NZ), ((0, 24),), -0.2, 0.2), 0.0, 2.0),
    }


def shift_plane(flat, step, depth):
    pos = lax.broadcasted_iota(jnp.int32, (flat.shape[-1],), 0) % depth
    inside = (pos + step >= 0) & (pos + step < depth)
    direct = jnp.roll(flat, -step, axis=-1)
    if step > 0:
        wrapped = jnp.roll(flat, depth - step, axis=-1)
    else:
        wrapped = jnp.roll(flat, -step - depth, axis=-1)
    return jnp.where(inside, direct, wrapped)


def plane_terms(center, depth):
    near = jnp.roll(center, -depth, axis=-1) + jnp.roll(center, depth, axis=-1)
    far = jnp.roll(center, -2 * depth, axis=-1) + jnp.roll(center, 2 * depth, axis=-1)
    near = near + shift_plane(center, 1, depth) + shift_plane(center, -1, depth)
    far = far + shift_plane(center, 2, depth) + shift_plane(center, -2, depth)
    return (4.0 / 3.0) * near - (1.0 / 12.0) * far


def apply_hamiltonian(field, potential):
    near = jnp.roll(field, 1, axis=1) + jnp.roll(field, -1, axis=1)
    far = jnp.roll(field, 2, axis=1) + jnp.roll(field, -2, axis=1)
    laplace = (4.0 / 3.0) * near - (1.0 / 12.0) * far + plane_terms(field, NZ) - 7.5 * field
    return -0.5 * laplace + potential[None] * field


def filter_block(block, potential):
    first = (apply_hamiltonian(block, potential) - 6.0 * block) / 4.0
    second = 2.0 * (apply_hamiltonian(first, potential) - 6.0 * first) / 4.0 - block
    return 2.0 * (apply_hamiltonian(second, potential) - 6.0 * second) / 4.0 - first


def reference(orbitals, potential):
    blocks = orbitals.reshape(N_BAND, ORBS // N_BAND, NX, NY * NZ)
    filtered = lax.map(lambda block: filter_block(block, potential), blocks).reshape(orbitals.shape)
    flat = filtered.reshape(ORBS, NX * NY * NZ)
    margin = jnp.dot(flat, flat.T, precision=lax.Precision.HIGHEST, preferred_element_type=jnp.float32)
    return filtered, margin * (1.0 / (NX * NY * NZ))
```

```python
import jax
import jax.numpy as jnp
from jax import lax
from jax.experimental import pallas as pl
from jax.experimental.pallas import tpu as pltpu
from jax.sharding import PartitionSpec as P

MESH = pl.DeviceIdType.MESH
NX_CHIPS, NZ_LO, NZ_HI, N_Y = 4, 6, 2, 8
N_Z = NZ_LO * NZ_HI
ROWS = 24
ORBS = 768
LANES = 128
TILES = ORBS // LANES
CELLS = 48 * 2048


def where_am_i():
    space, band = lax.axis_index("space"), lax.axis_index("band")
    x, z_lo = lax.div(space, NZ_LO), lax.rem(space, NZ_LO)
    core, pair = lax.rem(band, 2), lax.div(band, 2)
    y, z_hi = lax.rem(pair, N_Y), lax.div(pair, N_Y)
    return x, y, z_hi * NZ_LO + z_lo, core


def device(x, y, z, core):
    z_hi, z_lo = lax.div(z, NZ_LO), lax.rem(z, NZ_LO)
    return (x * NZ_LO + z_lo, (z_hi * N_Y + y) * 2 + core)


def margin_kernel(
    cells_ref, out_ref, held, rows, cat, part, ring, mine, pieces,
    meet_send, meet_recv, core_send, core_recv, ring_send, ring_recv,
    piece_send, piece_recv, out_send, out_recv,
):
    x, y, z, core = where_am_i()
    z_hi, z_lo = lax.div(z, NZ_LO), lax.rem(z, NZ_LO)
    band = (z_hi * N_Y + y) * 2 + core
    other = device(x, y, z, 1 - core)
    up = device(x, lax.rem(y + 1, N_Y), z, core)
    down = device(x, lax.rem(y + N_Y - 1, N_Y), z, core)
    half_z = NZ_LO // 2
    above, below = lax.rem(z + half_z, N_Z), lax.rem(z + N_Z - half_z, N_Z)
    spot = z_hi * 24 + x * NZ_LO + z_lo

    def spot_device(index):
        hi, rest = lax.div(index, 24), lax.rem(index, 24)
        return (rest, (hi * N_Y + y) * 2 + core)

    barrier = pltpu.get_barrier_semaphore()

    def greet(peer):
        pl.semaphore_signal(barrier, inc=1, device_id=peer, device_id_type=MESH)

    for peer in (other, up, down):
        greet(peer)

    def greet_meeting(k, carry):
        greet(device(x, k, above, core))
        greet(device(x, k, below, core))
        return carry

    lax.fori_loop(0, N_Y, greet_meeting, 0)

    def greet_spots(k, carry):
        greet(spot_device(lax.rem(spot + k, 48)))
        return carry

    lax.fori_loop(1, 48, greet_spots, 0)
    pl.semaphore_wait(barrier, 3 + 2 * N_Y + 47)

    def meeting(k, way):
        to_y = lax.rem(y + k, N_Y)
        to_z, plane = (above, z_hi) if way == 0 else (below, 1 - z_hi)
        return pltpu.make_async_remote_copy(
            src_ref=cells_ref.at[pl.ds(16 * plane + 2 * to_y, 2)],
            dst_ref=held.at[:, pl.ds(pl.multiple_of(ROWS * band, 8), ROWS), :],
            send_sem=meet_send.at[way, k],
            recv_sem=meet_recv.at[z_hi * N_Y + y],
            device_id=device(x, to_y, to_z, core),
            device_id_type=MESH,
        )

    def start_meeting(k, carry):
        meeting(k, 0).start()
        meeting(k, 1).start()
        return carry

    lax.fori_loop(0, N_Y, start_meeting, 0)

    def across(j):
        place = held.at[:, pl.ds(pl.multiple_of(ROWS * (2 * j + core), 8), ROWS), :]
        return pltpu.make_async_remote_copy(
            src_ref=place, dst_ref=place,
            send_sem=core_send.at[j], recv_sem=core_recv.at[j],
            device_id=other, device_id_type=MESH,
        )

    def arrived(k, carry):
        for hi in range(2):
            j = hi * N_Y + lax.rem(y + k, N_Y)
            place = held.at[:, pl.ds(pl.multiple_of(ROWS * (2 * j + core), 8), ROWS), :]
            pltpu.make_async_remote_copy(
                src_ref=place, dst_ref=place,
                send_sem=core_send.at[j], recv_sem=meet_recv.at[j],
                device_id=other, device_id_type=MESH,
            ).wait_recv()
            across(j).start()
        return carry

    lax.fori_loop(0, N_Y, arrived, 0)

    def crossed(j, carry):
        across(j).wait_recv()
        return carry

    lax.fori_loop(0, 2 * N_Y, crossed, 0)

    for g in range(2 * N_Y):
        for k in range(2):
            rows[g, :, LANES * k:LANES * (k + 1)] = held[
                k, pl.ds(pl.multiple_of(ROWS * (2 * g + core), 8), ROWS), :
            ]
    left = rows[...].reshape(2 * N_Y * ROWS, 2 * LANES)
    left_hi = left.astype(jnp.bfloat16)
    left_lo = (left - left_hi.astype(jnp.float32)).astype(jnp.bfloat16)
    left_cat = jnp.concatenate([left_hi, left_hi, left_lo], axis=1)
    for k in range(2):
        plane = held[k]
        hi = plane.astype(jnp.bfloat16)
        lo = (plane - hi.astype(jnp.float32)).astype(jnp.bfloat16)
        for slot, value in enumerate((hi, lo, hi)):
            cat[:, 2 * LANES * slot + LANES * k:2 * LANES * slot + LANES * (k + 1)] = value
    for n in range(3):
        block = lax.dot_general(
            left_cat, cat[256 * n:256 * (n + 1), :], (((1,), (1,)), ((), ())),
            preferred_element_type=jnp.float32,
        )
        part[:, :, :, 256 * n:256 * (n + 1)] = block.reshape(2, N_Y, ROWS, 256)

    def hop(way, step, h, source):
        return pltpu.make_async_remote_copy(
            src_ref=source,
            dst_ref=ring.at[way, step, h],
            send_sem=ring_send.at[way, step, h],
            recv_sem=ring_recv.at[way, step, h],
            device_id=up if way == 0 else down,
            device_id_type=MESH,
        )

    def goal(way, step):
        return lax.rem(y + (4 - step if way == 0 else N_Y - 4 + step), N_Y)

    for way in range(2):
        hop(way, 0, way, part.at[way, goal(way, 0)]).start()
    for way in range(2):
        hop(way, 1, 1 - way, part.at[1 - way, goal(way, 1)]).start()
    for step in range(4):
        for first in range(2):
            for way in range(2):
                h = way if (first == 1) == (step != 0) else 1 - way
                if step == 0 and first == 1:
                    continue
                if step == 0:
                    h = way
                slot = ring.at[way, step, h]
                hop(way, step, h, slot).wait_recv()
                if step < 3:
                    ring[way, step, h] = ring[way, step, h] + part[h, goal(way, step + 1)]
                    hop(way, step + 1, h, slot).start()

    for h in range(2):
        total = part[h, y] + ring[0, 3, h] + ring[1, 3, h]
        for t in range(TILES):
            mine[ROWS * h:ROWS * (h + 1), t, :] = total[:, LANES * t:LANES * (t + 1)]

    def piece(k):
        peer = lax.rem(spot + k, 48)
        return pltpu.make_async_remote_copy(
            src_ref=mine.at[peer], dst_ref=pieces.at[spot],
            send_sem=piece_send.at[k], recv_sem=piece_recv.at[spot],
            device_id=spot_device(peer), device_id_type=MESH,
        )

    def start_piece(k, carry):
        piece(k).start()
        return carry

    lax.fori_loop(1, 48, start_piece, 0)
    pieces[spot] = mine[spot]

    def wait_piece(k, carry):
        source = lax.rem(spot + k, 48)
        pltpu.make_async_remote_copy(
            src_ref=mine.at[source], dst_ref=pieces.at[source],
            send_sem=piece_send.at[k], recv_sem=piece_recv.at[source],
            device_id=spot_device(source), device_id_type=MESH,
        ).wait_recv()
        return carry

    lax.fori_loop(1, 48, wait_piece, 0)
    row = lax.rem(spot, 24)
    out_ref[row] = jnp.sum(pieces[...], axis=0) * (1.0 / CELLS)

    def give(k):
        peer = lax.rem(row + k, 24)
        return pltpu.make_async_remote_copy(
            src_ref=out_ref.at[row], dst_ref=out_ref.at[row],
            send_sem=out_send.at[k], recv_sem=out_recv.at[row],
            device_id=(peer, band), device_id_type=MESH,
        )

    def start_give(k, carry):
        give(k).start()
        return carry

    lax.fori_loop(1, 24, start_give, 0)

    def wait_give(k, carry):
        source = lax.rem(row + k, 24)
        pltpu.make_async_remote_copy(
            src_ref=out_ref.at[source], dst_ref=out_ref.at[source],
            send_sem=out_send.at[k], recv_sem=out_recv.at[source],
            device_id=(source, band), device_id_type=MESH,
        ).wait_recv()
        return carry

    lax.fori_loop(1, 24, wait_give, 0)

    def sent_meeting(k, carry):
        meeting(k, 0).wait_send()
        meeting(k, 1).wait_send()
        return carry

    lax.fori_loop(0, N_Y, sent_meeting, 0)

    def sent_across(j, carry):
        across(j).wait_send()
        return carry

    lax.fori_loop(0, 2 * N_Y, sent_across, 0)
    for way in range(2):
        for step in range(4):
            for h in range(2):
                if step > 0 or h == way:
                    hop(way, step, h, ring.at[way, step, h]).wait_send()

    def sent_piece(k, carry):
        piece(k).wait_send()
        return carry

    lax.fori_loop(1, 48, sent_piece, 0)

    def sent_give(k, carry):
        give(k).wait_send()
        return carry

    lax.fori_loop(1, 24, sent_give, 0)


def margin_of(filtered):
    cells = filtered.reshape(ROWS, 32, LANES).transpose(1, 0, 2)
    dma = pltpu.SemaphoreType.DMA
    out = pl.pallas_call(
        margin_kernel,
        out_shape=jax.ShapeDtypeStruct((ROWS, TILES, LANES), jnp.float32),
        in_specs=[pl.BlockSpec(memory_space=pltpu.VMEM)],
        out_specs=pl.BlockSpec(memory_space=pltpu.VMEM),
        scratch_shapes=[
            pltpu.VMEM((2, ORBS, LANES), jnp.float32),
            pltpu.VMEM((2 * N_Y, ROWS, 2 * LANES), jnp.float32),
            pltpu.VMEM((ORBS, 6 * LANES), jnp.bfloat16),
            pltpu.VMEM((2, N_Y, ROWS, ORBS), jnp.float32),
            pltpu.VMEM((2, 4, 2, ROWS, ORBS), jnp.float32),
            pltpu.VMEM((48, TILES, LANES), jnp.float32),
            pltpu.VMEM((48, TILES, LANES), jnp.float32),
            dma((2, N_Y)), dma((2 * N_Y,)), dma((2 * N_Y,)), dma((2 * N_Y,)),
            dma((2, 4, 2)), dma((2, 4, 2)), dma((48,)), dma((48,)), dma((24,)), dma((24,)),
        ],
        compiler_params=pltpu.CompilerParams(collective_id=0, has_side_effects=True),
    )(cells)
    return out.reshape(ROWS, ORBS)


NZ = 64


def padded_2(cells, sides, width):
    for axis, dim in sides:
        count = lax.axis_size(axis)
        head = lax.slice_in_dim(cells, 0, width, axis=dim)
        tail = lax.slice_in_dim(cells, cells.shape[dim] - width, cells.shape[dim], axis=dim)
        cells = jnp.concatenate(
            [
                lax.ppermute(tail, axis, [(i, (i + 1) % count) for i in range(count)]),
                cells,
                lax.ppermute(head, axis, [((i + 1) % count, i) for i in range(count)]),
            ],
            axis=dim,
        )
    return cells


def shift_plane(flat, step, depth):
    pos = lax.broadcasted_iota(jnp.int32, (flat.shape[-1],), 0) % depth
    inside = (pos + step >= 0) & (pos + step < depth)
    direct = jnp.roll(flat, -step, axis=-1)
    if step > 0:
        wrapped = jnp.roll(flat, depth - step, axis=-1)
    else:
        wrapped = jnp.roll(flat, -step - depth, axis=-1)
    return jnp.where(inside, direct, wrapped)


def plane_terms(center, depth):
    near = jnp.roll(center, -depth, axis=-1) + jnp.roll(center, depth, axis=-1)
    far = jnp.roll(center, -2 * depth, axis=-1) + jnp.roll(center, 2 * depth, axis=-1)
    near = near + shift_plane(center, 1, depth) + shift_plane(center, -1, depth)
    far = far + shift_plane(center, 2, depth) + shift_plane(center, -2, depth)
    return 4.0 / 3.0 * near - 1.0 / 12.0 * far


def apply_hamiltonian(field, potential):
    padded = padded_2(field, (("space", 1),), 2)
    center = padded[:, 2:-2]
    near = padded[:, 1:-3] + padded[:, 3:-1]
    far = padded[:, :-4] + padded[:, 4:]
    laplace = 4.0 / 3.0 * near - 1.0 / 12.0 * far + plane_terms(center, NZ) - 7.5 * center
    return -0.5 * laplace + potential[None] * center


def chebyshev(block, potential, operator):
    first = (operator(block, potential) - 6.0 * block) / 4.0
    second = 2.0 * (operator(first, potential) - 6.0 * first) / 4.0 - block
    return 2.0 * (operator(second, potential) - 6.0 * second) / 4.0 - first


def shards(orbitals, potential):
    filtered = chebyshev(orbitals, potential, apply_hamiltonian)
    return (filtered, margin_of(filtered))


def solution(mesh):
    return jax.shard_map(
        shards,
        mesh=mesh,
        in_specs=(P("band", "space", None), P("space", None)),
        out_specs=(P("band", "space", None), P("band", None)),
        check_vma=False,
    )
```

```python
import jax
import jax.numpy as jnp
from jax import lax
from jax.experimental import pallas as pl
from jax.experimental.pallas import tpu as pltpu
from jax.sharding import PartitionSpec as P

MESH = pl.DeviceIdType.MESH
NX_CHIPS, NZ_LO, NZ_HI, N_Y = 4, 6, 2, 8
N_Z = NZ_LO * NZ_HI
NZ = 64
ROWS = 24
ORBS = 768
LANES = 128
TILES = ORBS // LANES
CELLS = 48 * 2048


def where_am_i():
    space, band = lax.axis_index("space"), lax.axis_index("band")
    x, z_lo = lax.div(space, NZ_LO), lax.rem(space, NZ_LO)
    core, pair = lax.rem(band, 2), lax.div(band, 2)
    y, z_hi = lax.rem(pair, N_Y), lax.div(pair, N_Y)
    return x, y, z_hi * NZ_LO + z_lo, core


def device(x, y, z, core):
    z_hi, z_lo = lax.div(z, NZ_LO), lax.rem(z, NZ_LO)
    return (x * NZ_LO + z_lo, (z_hi * N_Y + y) * 2 + core)


def margin_kernel(
    cells_ref, out_ref, held, rows, cat, part, ring, mine, pieces,
    meet_send, meet_recv, core_send, core_recv, ring_send, ring_recv,
    piece_send, piece_recv, out_send, out_recv,
):
    x, y, z, core = where_am_i()
    z_hi, z_lo = lax.div(z, NZ_LO), lax.rem(z, NZ_LO)
    band = (z_hi * N_Y + y) * 2 + core
    other = device(x, y, z, 1 - core)
    up = device(x, lax.rem(y + 1, N_Y), z, core)
    down = device(x, lax.rem(y + N_Y - 1, N_Y), z, core)
    half_z = NZ_LO // 2
    above, below = lax.rem(z + half_z, N_Z), lax.rem(z + N_Z - half_z, N_Z)
    spot = z_hi * 24 + x * NZ_LO + z_lo

    def spot_device(index):
        hi, rest = lax.div(index, 24), lax.rem(index, 24)
        return (rest, (hi * N_Y + y) * 2 + core)

    barrier = pltpu.get_barrier_semaphore()

    def greet(peer):
        pl.semaphore_signal(barrier, inc=1, device_id=peer, device_id_type=MESH)

    for peer in (other, up, down):
        greet(peer)

    def greet_meeting(k, carry):
        greet(device(x, k, above, core))
        greet(device(x, k, below, core))
        return carry

    lax.fori_loop(0, N_Y, greet_meeting, 0)

    def greet_spots(k, carry):
        greet(spot_device(lax.rem(spot + k, 48)))
        return carry

    lax.fori_loop(1, 48, greet_spots, 0)
    pl.semaphore_wait(barrier, 3 + 2 * N_Y + 47)

    def meeting(k, way):
        to_y = lax.rem(y + k, N_Y)
        to_z, plane = (above, z_hi) if way == 0 else (below, 1 - z_hi)
        return pltpu.make_async_remote_copy(
            src_ref=cells_ref.at[pl.ds(16 * plane + 2 * to_y, 2)],
            dst_ref=held.at[:, pl.ds(pl.multiple_of(ROWS * band, 8), ROWS), :],
            send_sem=meet_send.at[way, k],
            recv_sem=meet_recv.at[z_hi * N_Y + y],
            device_id=device(x, to_y, to_z, core),
            device_id_type=MESH,
        )

    def start_meeting(k, carry):
        meeting(k, 0).start()
        meeting(k, 1).start()
        return carry

    lax.fori_loop(0, N_Y, start_meeting, 0)

    def across(j):
        place = held.at[:, pl.ds(pl.multiple_of(ROWS * (2 * j + core), 8), ROWS), :]
        return pltpu.make_async_remote_copy(
            src_ref=place, dst_ref=place,
            send_sem=core_send.at[j], recv_sem=core_recv.at[j],
            device_id=other, device_id_type=MESH,
        )

    def arrived(k, carry):
        for hi in range(2):
            j = hi * N_Y + lax.rem(y + k, N_Y)
            place = held.at[:, pl.ds(pl.multiple_of(ROWS * (2 * j + core), 8), ROWS), :]
            pltpu.make_async_remote_copy(
                src_ref=place, dst_ref=place,
                send_sem=core_send.at[j], recv_sem=meet_recv.at[j],
                device_id=other, device_id_type=MESH,
            ).wait_recv()
            across(j).start()
        return carry

    lax.fori_loop(0, N_Y, arrived, 0)

    def crossed(j, carry):
        across(j).wait_recv()
        return carry

    lax.fori_loop(0, 2 * N_Y, crossed, 0)

    for g in range(2 * N_Y):
        for k in range(2):
            rows[g, :, LANES * k:LANES * (k + 1)] = held[
                k, pl.ds(pl.multiple_of(ROWS * (2 * g + core), 8), ROWS), :
            ]
    left = rows[...].reshape(2 * N_Y * ROWS, 2 * LANES)
    left_hi = left.astype(jnp.bfloat16)
    left_lo = (left - left_hi.astype(jnp.float32)).astype(jnp.bfloat16)
    left_cat = jnp.concatenate([left_hi, left_hi, left_lo], axis=1)
    for k in range(2):
        plane = held[k]
        hi = plane.astype(jnp.bfloat16)
        lo = (plane - hi.astype(jnp.float32)).astype(jnp.bfloat16)
        for slot, value in enumerate((hi, lo, hi)):
            cat[:, 2 * LANES * slot + LANES * k:2 * LANES * slot + LANES * (k + 1)] = value
    for n in range(3):
        block = lax.dot_general(
            left_cat, cat[256 * n:256 * (n + 1), :], (((1,), (1,)), ((), ())),
            preferred_element_type=jnp.float32,
        )
        part[:, :, :, 256 * n:256 * (n + 1)] = block.reshape(2, N_Y, ROWS, 256)

    def hop(way, step, h, source):
        return pltpu.make_async_remote_copy(
            src_ref=source,
            dst_ref=ring.at[way, step, h],
            send_sem=ring_send.at[way, step, h],
            recv_sem=ring_recv.at[way, step, h],
            device_id=up if way == 0 else down,
            device_id_type=MESH,
        )

    def goal(way, step):
        return lax.rem(y + (4 - step if way == 0 else N_Y - 4 + step), N_Y)

    for way in range(2):
        hop(way, 0, way, part.at[way, goal(way, 0)]).start()
    for way in range(2):
        hop(way, 1, 1 - way, part.at[1 - way, goal(way, 1)]).start()
    for step in range(4):
        for first in range(2):
            for way in range(2):
                h = way if (first == 1) == (step != 0) else 1 - way
                if step == 0 and first == 1:
                    continue
                if step == 0:
                    h = way
                slot = ring.at[way, step, h]
                hop(way, step, h, slot).wait_recv()
                if step < 3:
                    ring[way, step, h] = ring[way, step, h] + part[h, goal(way, step + 1)]
                    hop(way, step + 1, h, slot).start()

    for h in range(2):
        total = part[h, y] + ring[0, 3, h] + ring[1, 3, h]
        for t in range(TILES):
            mine[ROWS * h:ROWS * (h + 1), t, :] = total[:, LANES * t:LANES * (t + 1)]

    def piece(k):
        peer = lax.rem(spot + k, 48)
        return pltpu.make_async_remote_copy(
            src_ref=mine.at[peer], dst_ref=pieces.at[spot],
            send_sem=piece_send.at[k], recv_sem=piece_recv.at[spot],
            device_id=spot_device(peer), device_id_type=MESH,
        )

    def start_piece(k, carry):
        piece(k).start()
        return carry

    lax.fori_loop(1, 48, start_piece, 0)
    pieces[spot] = mine[spot]

    def wait_piece(k, carry):
        source = lax.rem(spot + k, 48)
        pltpu.make_async_remote_copy(
            src_ref=mine.at[source], dst_ref=pieces.at[source],
            send_sem=piece_send.at[k], recv_sem=piece_recv.at[source],
            device_id=spot_device(source), device_id_type=MESH,
        ).wait_recv()
        return carry

    lax.fori_loop(1, 48, wait_piece, 0)
    row = lax.rem(spot, 24)
    out_ref[row] = jnp.sum(pieces[...], axis=0) * (1.0 / CELLS)

    def give(k):
        peer = lax.rem(row + k, 24)
        return pltpu.make_async_remote_copy(
            src_ref=out_ref.at[row], dst_ref=out_ref.at[row],
            send_sem=out_send.at[k], recv_sem=out_recv.at[row],
            device_id=(peer, band), device_id_type=MESH,
        )

    def start_give(k, carry):
        give(k).start()
        return carry

    lax.fori_loop(1, 24, start_give, 0)

    def wait_give(k, carry):
        source = lax.rem(row + k, 24)
        pltpu.make_async_remote_copy(
            src_ref=out_ref.at[source], dst_ref=out_ref.at[source],
            send_sem=out_send.at[k], recv_sem=out_recv.at[source],
            device_id=(source, band), device_id_type=MESH,
        ).wait_recv()
        return carry

    lax.fori_loop(1, 24, wait_give, 0)

    def sent_meeting(k, carry):
        meeting(k, 0).wait_send()
        meeting(k, 1).wait_send()
        return carry

    lax.fori_loop(0, N_Y, sent_meeting, 0)

    def sent_across(j, carry):
        across(j).wait_send()
        return carry

    lax.fori_loop(0, 2 * N_Y, sent_across, 0)
    for way in range(2):
        for step in range(4):
            for h in range(2):
                if step > 0 or h == way:
                    hop(way, step, h, ring.at[way, step, h]).wait_send()

    def sent_piece(k, carry):
        piece(k).wait_send()
        return carry

    lax.fori_loop(1, 48, sent_piece, 0)

    def sent_give(k, carry):
        give(k).wait_send()
        return carry

    lax.fori_loop(1, 24, sent_give, 0)


def margin_of(filtered):
    cells = filtered.reshape(ROWS, 32, LANES).transpose(1, 0, 2)
    dma = pltpu.SemaphoreType.DMA
    out = pl.pallas_call(
        margin_kernel,
        out_shape=jax.ShapeDtypeStruct((ROWS, TILES, LANES), jnp.float32),
        in_specs=[pl.BlockSpec(memory_space=pltpu.VMEM)],
        out_specs=pl.BlockSpec(memory_space=pltpu.VMEM),
        scratch_shapes=[
            pltpu.VMEM((2, ORBS, LANES), jnp.float32),
            pltpu.VMEM((2 * N_Y, ROWS, 2 * LANES), jnp.float32),
            pltpu.VMEM((ORBS, 6 * LANES), jnp.bfloat16),
            pltpu.VMEM((2, N_Y, ROWS, ORBS), jnp.float32),
            pltpu.VMEM((2, 4, 2, ROWS, ORBS), jnp.float32),
            pltpu.VMEM((48, TILES, LANES), jnp.float32),
            pltpu.VMEM((48, TILES, LANES), jnp.float32),
            dma((2, N_Y)), dma((2 * N_Y,)), dma((2 * N_Y,)), dma((2 * N_Y,)),
            dma((2, 4, 2)), dma((2, 4, 2)), dma((48,)), dma((48,)), dma((24,)), dma((24,)),
        ],
        compiler_params=pltpu.CompilerParams(collective_id=0, has_side_effects=True),
    )(cells)
    return out.reshape(ROWS, ORBS)


def filter_kernel(
    orbs_ref, pot_ref, home_ref, field, first, second, last, pot,
    in_send, in_recv, pot_send, pot_recv, share_send, share_recv, back_send, back_recv,
):
    x, y, z, core = where_am_i()
    z_hi, z_lo = lax.div(z, NZ_LO), lax.rem(z, NZ_LO)
    band = (z_hi * N_Y + y) * 2 + core
    me = x * NZ_LO + z_lo
    quarter = lax.rem(y, 2) * 2 + core
    tile = lax.rem(quarter, 2)
    plane = lax.div(quarter, 2)

    def friend(k):
        q = lax.rem(quarter + k, 4)
        return q, (me, (z_hi * N_Y + lax.div(y, 2) * 2 + lax.div(q, 2)) * 2 + lax.rem(q, 2))

    barrier = pltpu.get_barrier_semaphore()

    def greet(k, carry):
        pl.semaphore_signal(
            barrier, inc=1, device_id=(lax.rem(me + k, 24), band), device_id_type=MESH
        )
        return carry

    lax.fori_loop(1, 24, greet, 0)
    for k in range(1, 4):
        pl.semaphore_signal(barrier, inc=1, device_id=friend(k)[1], device_id_type=MESH)
    pl.semaphore_wait(barrier, 26)

    def pot_piece(source, q):
        return pot.at[2 * source + lax.div(q, 2), pl.ds(pl.multiple_of(8 * lax.rem(q, 2), 8), 8)]

    def pot_copy(k, source):
        return pltpu.make_async_remote_copy(
            src_ref=pot_ref.at[plane, pl.ds(pl.multiple_of(8 * tile, 8), 8)],
            dst_ref=pot_piece(source, quarter),
            send_sem=pot_send.at[k], recv_sem=pot_recv.at[source],
            device_id=(lax.rem(me + k, 24), band), device_id_type=MESH,
        )

    def in_copy(k, source):
        peer = lax.rem(me + k, 24)
        return pltpu.make_async_remote_copy(
            src_ref=orbs_ref.at[peer], dst_ref=field.at[pl.ds(2 + 2 * source, 2)],
            send_sem=in_send.at[k], recv_sem=in_recv.at[source],
            device_id=(peer, band), device_id_type=MESH,
        )

    def start_pot(k, carry):
        pot_copy(k, me).start()
        return carry

    lax.fori_loop(1, 24, start_pot, 0)

    def start_in(k, carry):
        in_copy(k, me).start()
        return carry

    lax.fori_loop(1, 24, start_in, 0)
    field[pl.ds(2 + 2 * me, 2)] = orbs_ref[me]
    pot[2 * me + plane, pl.ds(pl.multiple_of(8 * tile, 8), 8)] = pot_ref[
        plane, pl.ds(pl.multiple_of(8 * tile, 8), 8)
    ]

    def wait_pot(k, carry):
        pot_copy(k, lax.rem(me + k, 24)).wait_recv()
        return carry

    lax.fori_loop(1, 24, wait_pot, 0)

    def share(k, q):
        place = pot4.at[:, lax.div(q, 2), pl.ds(pl.multiple_of(8 * lax.rem(q, 2), 8), 8)]
        return pltpu.make_async_remote_copy(
            src_ref=place, dst_ref=place,
            send_sem=share_send.at[k], recv_sem=share_recv.at[q],
            device_id=friend(k)[1], device_id_type=MESH,
        )

    pot4 = pot.reshape(24, 2, 16, LANES)
    for k in range(1, 4):
        share(k, quarter).start()

    def wait_in(k, carry):
        in_copy(k, lax.rem(me + k, 24)).wait_recv()
        return carry

    lax.fori_loop(1, 24, wait_in, 0)
    for k in range(1, 4):
        share(k, friend(k)[0]).wait_recv()

    lane = lax.broadcasted_iota(jnp.int32, (4, 16, LANES), 2)
    even = lane < NZ
    deep = lax.rem(lane, NZ)

    def applied(source, at):
        center = source[pl.ds(at + 2, 4)]
        near = source[pl.ds(at + 1, 4)] + source[pl.ds(at + 3, 4)]
        far = source[pl.ds(at, 4)] + source[pl.ds(at + 4, 4)]
        swap = pltpu.roll(center, NZ, axis=2)
        near = near + swap + jnp.where(even, pltpu.roll(swap, 1, axis=1), pltpu.roll(swap, 15, axis=1))
        far = far + pltpu.roll(center, 1, axis=1) + pltpu.roll(center, 15, axis=1)
        near = near + pltpu.roll(jnp.where(deep == 0, swap, center), LANES - 1, axis=2)
        near = near + pltpu.roll(jnp.where(deep == NZ - 1, swap, center), 1, axis=2)
        far = far + pltpu.roll(jnp.where(deep < 2, swap, center), LANES - 2, axis=2)
        far = far + pltpu.roll(jnp.where(deep >= NZ - 2, swap, center), 2, axis=2)
        level = (pot[pl.ds(at, 4)] - 2.25) * 0.25
        return level * center - near * (1.0 / 6.0) + far * (1.0 / 96.0)

    def wrapped(target):
        target[0:2] = target[48:50]
        target[50:52] = target[2:4]

    wrapped(field)

    def stage_1(i, carry):
        first[pl.ds(4 * i + 2, 4)] = applied(field, 4 * i)
        return carry

    lax.fori_loop(0, 12, stage_1, 0)
    wrapped(first)

    def stage_2(i, carry):
        second[pl.ds(4 * i + 2, 4)] = 2.0 * applied(first, 4 * i) - field[pl.ds(4 * i + 2, 4)]
        return carry

    lax.fori_loop(0, 12, stage_2, 0)
    wrapped(second)

    def stage_3(i, carry):
        last[pl.ds(4 * i, 4)] = 2.0 * applied(second, 4 * i) - first[pl.ds(4 * i + 2, 4)]
        return carry

    lax.fori_loop(0, 12, stage_3, 0)

    def back_copy(k, orbital):
        peer = lax.rem(me + k, 24)
        return pltpu.make_async_remote_copy(
            src_ref=last.at[pl.ds(2 * peer, 2)], dst_ref=home_ref.at[orbital],
            send_sem=back_send.at[k], recv_sem=back_recv.at[orbital],
            device_id=(peer, band), device_id_type=MESH,
        )

    def start_back(k, carry):
        back_copy(k, me).start()
        return carry

    lax.fori_loop(1, 24, start_back, 0)
    home_ref[me] = last[pl.ds(2 * me, 2)]

    def finish(k, carry):
        back_copy(k, lax.rem(me + k, 24)).wait_recv()
        return carry

    lax.fori_loop(1, 24, finish, 0)

    def sent(k, carry):
        pot_copy(k, me).wait_send()
        in_copy(k, me).wait_send()
        back_copy(k, me).wait_send()
        return carry

    lax.fori_loop(1, 24, sent, 0)
    for k in range(1, 4):
        share(k, quarter).wait_send()


def filtered_of(orbitals, potential):
    dma = pltpu.SemaphoreType.DMA
    padded = pltpu.VMEM((52, 16, LANES), jnp.float32)
    vmem = pl.BlockSpec(memory_space=pltpu.VMEM)
    return pl.pallas_call(
        filter_kernel,
        out_shape=jax.ShapeDtypeStruct((ROWS, 2, 16, LANES), jnp.float32),
        in_specs=[vmem, vmem],
        out_specs=vmem,
        scratch_shapes=[
            padded, padded, padded,
            pltpu.VMEM((48, 16, LANES), jnp.float32), pltpu.VMEM((48, 16, LANES), jnp.float32),
            dma((24,)), dma((24,)), dma((24,)), dma((24,)), dma((4,)), dma((4,)), dma((24,)), dma((24,)),
        ],
        compiler_params=pltpu.CompilerParams(collective_id=1, has_side_effects=True),
    )(orbitals.reshape(ROWS, 2, 16, LANES), potential.reshape(2, 16, LANES))


def shards(orbitals, potential):
    filtered = filtered_of(orbitals, potential).reshape(ROWS, 2, 2048)
    return (filtered, margin_of(filtered))


def solution(mesh):
    return jax.shard_map(
        shards,
        mesh=mesh,
        in_specs=(P("band", "space", None), P("space", None)),
        out_specs=(P("band", "space", None), P("band", None)),
        check_vma=False,
    )
```

```python
import jax
import jax.numpy as jnp
from jax import lax
from jax.experimental import pallas as pl
from jax.experimental.pallas import tpu as pltpu
from jax.sharding import PartitionSpec as P

MESH = pl.DeviceIdType.MESH
NZ_LO, N_Y = 6, 8
SPACE = 24
SPOTS = 2 * SPACE
NZ = 64
ROWS = 24
ORBS = 768
LANES = 128
TILES = ORBS // LANES
CELLS = 48 * 2048


def kernel(
    orbs_ref, pot_ref, home_ref, margin_ref,
    field, first, second, last, pot, column, held, rows, cat, part, ring, mine, pieces, done,
    in_send, in_recv, pot_send, pot_recv, share_send, share_recv, col_send, col_recv,
    meet_send, meet_recv, core_send, core_recv, home_send, home_recv,
    ring_send, ring_recv, piece_send, piece_recv, out_send, out_recv,
):
    me, band = lax.axis_index("space"), lax.axis_index("band")
    core, pair = lax.rem(band, 2), lax.div(band, 2)
    y, z_hi = lax.rem(pair, N_Y), lax.div(pair, N_Y)
    spot = z_hi * SPACE + me
    seat = 2 * y + core

    def band_of(hi, a_y):
        return (hi * N_Y + a_y) * 2 + core

    def spot_device(index):
        return (lax.rem(index, SPACE), band_of(lax.div(index, SPACE), y))

    def seat_device(index):
        return (me, z_hi * 2 * N_Y + index)

    other = seat_device(2 * y + 1 - core)
    up = (me, band_of(z_hi, lax.rem(y + 1, N_Y)))
    down = (me, band_of(z_hi, lax.rem(y + N_Y - 1, N_Y)))

    def copy(source, target, send, recv, peer):
        return pltpu.make_async_remote_copy(
            src_ref=source, dst_ref=target, send_sem=send, recv_sem=recv,
            device_id=peer, device_id_type=MESH,
        )

    def each(low, high, body):
        def step(k, carry):
            body(k)
            return carry

        lax.fori_loop(low, high, step, 0)

    barrier = pltpu.get_barrier_semaphore()

    def greet(peer):
        pl.semaphore_signal(barrier, inc=1, device_id=peer, device_id_type=MESH)

    each(1, SPOTS, lambda k: greet(spot_device(lax.rem(spot + k, SPOTS))))
    each(1, 2 * N_Y, lambda k: greet(seat_device(lax.rem(seat + k, 2 * N_Y))))
    pl.semaphore_wait(barrier, SPOTS - 1 + 2 * N_Y - 1)

    def pot_copy(k, source):
        peer = lax.rem(me + k, SPACE)
        return copy(
            pot_ref.at[pl.ds(2 * seat, 2)], pot.at[source, pl.ds(2 * seat, 2)],
            pot_send.at[k], pot_recv.at[source], (peer, band),
        )

    def in_copy(k, source):
        peer = lax.rem(me + k, SPACE)
        return copy(
            orbs_ref.at[peer], field.at[1 + source],
            in_send.at[k], in_recv.at[source], (peer, band),
        )

    each(1, SPACE, lambda k: pot_copy(k, me).start())
    each(1, SPACE, lambda k: in_copy(k, me).start())
    field[1 + me] = orbs_ref[me]
    own_pot = pltpu.make_async_copy(
        pot_ref.at[pl.ds(2 * seat, 2)], pot.at[me, pl.ds(2 * seat, 2)], pot_recv.at[me]
    )
    own_pot.start()
    each(1, SPACE, lambda k: pot_copy(k, lax.rem(me + k, SPACE)).wait_recv())
    own_pot.wait()

    def share(k, source):
        place = pot.at[:, pl.ds(2 * source, 2)]
        return copy(
            place, place, share_send.at[k], share_recv.at[source],
            seat_device(lax.rem(seat + k, 2 * N_Y)),
        )

    each(1, 2 * N_Y, lambda k: share(k, seat).start())
    each(1, SPACE, lambda k: in_copy(k, lax.rem(me + k, SPACE)).wait_recv())
    each(1, 2 * N_Y, lambda k: share(k, lax.rem(seat + k, 2 * N_Y)).wait_recv())

    lane = lax.broadcasted_iota(jnp.int32, (2, 32, LANES), 2)
    row = lax.broadcasted_iota(jnp.int32, (2, 32, LANES), 1)
    low_half = lane < NZ
    deep = lax.rem(lane, NZ)
    low_plane = lax.rem(row, 2) == 0

    def applied(source, at):
        center = source[pl.ds(at + 1, 2)]
        before = source[pl.ds(at, 2)]
        after = source[pl.ds(at + 2, 2)]
        swap = pltpu.roll(center, NZ, axis=2)
        near = jnp.where(
            low_plane,
            pltpu.roll(center + before, 31, axis=1),
            pltpu.roll(center + after, 1, axis=1),
        )
        far = before + after
        near = near + swap + jnp.where(
            low_half, pltpu.roll(swap, 2, axis=1), pltpu.roll(swap, 30, axis=1)
        )
        far = far + pltpu.roll(center, 2, axis=1) + pltpu.roll(center, 30, axis=1)
        near = near + pltpu.roll(jnp.where(deep == 0, swap, center), LANES - 1, axis=2)
        near = near + pltpu.roll(jnp.where(deep == NZ - 1, swap, center), 1, axis=2)
        far = far + pltpu.roll(jnp.where(deep < 2, swap, center), LANES - 2, axis=2)
        far = far + pltpu.roll(jnp.where(deep >= NZ - 2, swap, center), 2, axis=2)
        level = (pot[pl.ds(at, 2)] - 2.25) * 0.25
        return level * center - near * (1.0 / 6.0) + far * (1.0 / 96.0)

    def wrapped(target):
        target[0] = target[SPACE]
        target[SPACE + 1] = target[1]

    def stage_1(i):
        first[pl.ds(2 * i + 1, 2)] = applied(field, 2 * i)

    def stage_2(i):
        second[pl.ds(2 * i + 1, 2)] = 2.0 * applied(first, 2 * i) - field[pl.ds(2 * i + 1, 2)]

    def stage_3(i):
        last[pl.ds(2 * i, 2)] = 2.0 * applied(second, 2 * i) - first[pl.ds(2 * i + 1, 2)]

    wrapped(field)
    each(0, 12, stage_1)
    wrapped(first)
    each(0, 12, stage_2)
    wrapped(second)
    each(0, 12, stage_3)

    def col_copy(tile, k, source):
        peer = lax.rem(spot + k, SPOTS)
        return copy(
            last.at[
                lax.rem(peer, SPACE),
                pl.ds(pl.multiple_of(16 * lax.div(peer, SPACE) + 8 * tile, 8), 8),
            ],
            column.at[lax.div(source, SPACE), lax.rem(source, SPACE), pl.ds(8 * tile, 8)],
            col_send.at[tile, k], col_recv.at[tile, source], spot_device(peer),
        )

    for tile in range(2):
        each(1, SPOTS, lambda k: col_copy(tile, k, spot).start())
    column[z_hi, me] = last[me, pl.ds(pl.multiple_of(16 * z_hi, 8), 16)]
    home_ref[me] = last[me]

    def band_place(k, hi, a_y):
        return held.at[k, pl.ds(pl.multiple_of(ROWS * band_of(hi, a_y), 8), ROWS)]

    def meet_copy(k, hi, a_y, source):
        return copy(
            column.at[hi, :, 8 * lax.rem(a_y, 2) + 2 * lax.div(a_y, 2) + k],
            band_place(k, hi, source),
            meet_send.at[hi, k, a_y], meet_recv.at[hi, k, source],
            (me, band_of(z_hi, a_y)),
        )

    def own_copy(k, hi):
        return pltpu.make_async_copy(
            column.at[hi, :, 8 * lax.rem(y, 2) + 2 * lax.div(y, 2) + k],
            band_place(k, hi, y), meet_recv.at[hi, k, y],
        )

    for tile in range(2):
        each(1, SPOTS, lambda k: col_copy(tile, k, lax.rem(spot + k, SPOTS)).wait_recv())

        def meet(i):
            a_y = 2 * lax.rem(lax.div(y, 2) + i, 4) + tile

            @pl.when(a_y != y)
            def _():
                for hi in range(2):
                    for k in range(2):
                        meet_copy(k, hi, a_y, y).start()

            @pl.when(a_y == y)
            def _():
                for hi in range(2):
                    for k in range(2):
                        own_copy(k, hi).start()

        each(0, 4, meet)

    def home_copy(k, orbital):
        peer = lax.rem(me + k, SPACE)
        return copy(
            last.at[peer], home_ref.at[orbital],
            home_send.at[k], home_recv.at[orbital], (peer, band),
        )

    each(1, SPACE, lambda k: home_copy(k, me).start())

    def across(j, a_core):
        place = held.at[:, pl.ds(pl.multiple_of(ROWS * (2 * j + a_core), 8), ROWS)]
        return copy(place, place, core_send.at[j], core_recv.at[j], other)

    for hi in range(2):
        for k in range(2):
            own_copy(k, hi).wait()
        across(hi * N_Y + y, core).start()

    def arrived(i):
        source = lax.rem(y + i, N_Y)
        for hi in range(2):
            for k in range(2):
                meet_copy(k, hi, source, source).wait_recv()
            across(hi * N_Y + source, core).start()

    each(1, N_Y, arrived)
    each(0, 2 * N_Y, lambda j: across(j, 1 - core).wait_recv())

    for g in range(2 * N_Y):
        for k in range(2):
            rows[g, :, LANES * k:LANES * (k + 1)] = held[
                k, pl.ds(pl.multiple_of(ROWS * (2 * g + core), 8), ROWS), :
            ]
    left = rows[...].reshape(2 * N_Y * ROWS, 2 * LANES)
    left_hi = left.astype(jnp.bfloat16)
    left_lo = (left - left_hi.astype(jnp.float32)).astype(jnp.bfloat16)
    left_cat = jnp.concatenate([left_hi, left_hi, left_lo], axis=1)
    for k in range(2):
        cells = held[k]
        cells_hi = cells.astype(jnp.bfloat16)
        cells_lo = (cells - cells_hi.astype(jnp.float32)).astype(jnp.bfloat16)
        for slot, value in enumerate((cells_hi, cells_lo, cells_hi)):
            cat[:, 2 * LANES * slot + LANES * k:2 * LANES * slot + LANES * (k + 1)] = value
    for n in range(3):
        block = lax.dot_general(
            left_cat, cat[256 * n:256 * (n + 1), :], (((1,), (1,)), ((), ())),
            preferred_element_type=jnp.float32,
        )
        part[:, :, :, 256 * n:256 * (n + 1)] = block.reshape(2, N_Y, ROWS, 256)

    def hop(way, step, h, source):
        return copy(
            source, ring.at[way, step, h],
            ring_send.at[way, step, h], ring_recv.at[way, step, h], up if way == 0 else down,
        )

    def goal(way, step):
        return lax.rem(y + (4 - step if way == 0 else N_Y - 4 + step), N_Y)

    for way in range(2):
        hop(way, 0, way, part.at[way, goal(way, 0)]).start()
    for way in range(2):
        hop(way, 1, 1 - way, part.at[1 - way, goal(way, 1)]).start()
    for step in range(4):
        for turn in range(2 if step else 1):
            for way in range(2):
                h = way if turn == 1 or step == 0 else 1 - way
                slot = ring.at[way, step, h]
                hop(way, step, h, slot).wait_recv()
                if step < 3:
                    ring[way, step, h] = ring[way, step, h] + part[h, goal(way, step + 1)]
                    hop(way, step + 1, h, slot).start()

    for h in range(2):
        total = part[h, y] + ring[0, 3, h] + ring[1, 3, h]
        for t in range(TILES):
            mine[ROWS * h:ROWS * (h + 1), t, :] = total[:, LANES * t:LANES * (t + 1)]

    def piece(k, source):
        peer = lax.rem(spot + k, SPOTS)
        return copy(
            mine.at[peer], pieces.at[source],
            piece_send.at[k], piece_recv.at[source], spot_device(peer),
        )

    each(1, SPOTS, lambda k: piece(k, spot).start())
    pieces[spot] = mine[spot]
    each(1, SPOTS, lambda k: piece(k, lax.rem(spot + k, SPOTS)).wait_recv())
    done[me] = jnp.sum(pieces[...], axis=0) * (1.0 / CELLS)

    def give(k, source):
        peer = lax.rem(me + k, SPACE)
        return copy(
            done.at[me], done.at[source], out_send.at[k], out_recv.at[source], (peer, band)
        )

    each(1, SPACE, lambda k: give(k, me).start())
    each(1, SPACE, lambda k: give(k, lax.rem(me + k, SPACE)).wait_recv())
    for t in range(TILES):
        margin_ref[:, LANES * t:LANES * (t + 1)] = done[:, t, :]

    def finish(k):
        home_copy(k, lax.rem(me + k, SPACE)).wait_recv()
        for sent in (pot_copy, in_copy, home_copy, give):
            sent(k, me).wait_send()

    each(1, SPACE, finish)
    each(1, 2 * N_Y, lambda k: share(k, seat).wait_send())

    def finish_spots(k):
        for tile in range(2):
            col_copy(tile, k, spot).wait_send()
        piece(k, spot).wait_send()

    each(1, SPOTS, finish_spots)

    def finish_meet(i):
        for hi in range(2):
            for k in range(2):
                meet_copy(k, hi, lax.rem(y + i, N_Y), y).wait_send()

    each(1, N_Y, finish_meet)
    each(0, 2 * N_Y, lambda j: across(j, core).wait_send())
    for way in range(2):
        for step in range(4):
            for h in range(2):
                if step > 0 or h == way:
                    hop(way, step, h, ring.at[way, step, h]).wait_send()


def shards(orbitals, potential):
    dma = pltpu.SemaphoreType.DMA
    f32 = jnp.float32
    vmem = pl.BlockSpec(memory_space=pltpu.VMEM)
    padded = pltpu.VMEM((SPACE + 2, 32, LANES), f32)
    home, margin = pl.pallas_call(
        kernel,
        out_shape=(
            jax.ShapeDtypeStruct((ROWS, 32, LANES), f32),
            jax.ShapeDtypeStruct((ROWS, ORBS), f32),
        ),
        in_specs=[vmem, vmem],
        out_specs=(vmem, vmem),
        scratch_shapes=[
            padded, padded, padded,
            pltpu.VMEM((SPACE, 32, LANES), f32),
            pltpu.VMEM((SPACE, 32, LANES), f32),
            pltpu.VMEM((2, SPACE, 16, LANES), f32),
            pltpu.VMEM((2, ORBS, LANES), f32),
            pltpu.VMEM((2 * N_Y, ROWS, 2 * LANES), f32),
            pltpu.VMEM((ORBS, 6 * LANES), jnp.bfloat16),
            pltpu.VMEM((2, N_Y, ROWS, ORBS), f32),
            pltpu.VMEM((2, 4, 2, ROWS, ORBS), f32),
            pltpu.VMEM((SPOTS, TILES, LANES), f32),
            pltpu.VMEM((SPOTS, TILES, LANES), f32),
            pltpu.VMEM((ROWS, TILES, LANES), f32),
            dma((SPACE,)), dma((SPACE,)), dma((SPACE,)), dma((SPACE,)),
            dma((2 * N_Y,)), dma((2 * N_Y,)), dma((2, SPOTS)), dma((2, SPOTS)),
            dma((2, 2, N_Y)), dma((2, 2, N_Y)), dma((2 * N_Y,)), dma((2 * N_Y,)),
            dma((SPACE,)), dma((SPACE,)),
            dma((2, 4, 2)), dma((2, 4, 2)), dma((SPOTS,)), dma((SPOTS,)), dma((SPACE,)), dma((SPACE,)),
        ],
        compiler_params=pltpu.CompilerParams(collective_id=0, has_side_effects=True),
    )(
        orbitals.reshape(ROWS, 2, 16, LANES).transpose(0, 2, 1, 3).reshape(ROWS, 32, LANES),
        potential.reshape(2, 16, LANES).transpose(1, 0, 2).reshape(32, LANES),
    )
    filtered = home.reshape(ROWS, 16, 2, LANES).transpose(0, 2, 1, 3).reshape(ROWS, 2, 2048)
    return (filtered, margin)


def solution(mesh):
    return jax.shard_map(
        shards,
        mesh=mesh,
        in_specs=(P("band", "space", None), P("space", None)),
        out_specs=(P("band", "space", None), P("band", None)),
        check_vma=False,
    )
```

```python
import jax
import jax.numpy as jnp
from jax import lax
from jax.experimental import pallas as pl
from jax.experimental.pallas import tpu as pltpu
from jax.sharding import PartitionSpec as P

MESH = pl.DeviceIdType.MESH
NZ_LO, N_Y = 6, 8
SPACE = 24
SPOTS = 2 * SPACE
NZ = 64
ROWS = 24
ORBS = 768
LANES = 128
TILES = ORBS // LANES
CELLS = 48 * 2048
EARLY = 24


def kernel(
    orbs_ref, pot_ref, home_ref, margin_ref,
    field, first, second, last, pot, column, held, rows, cat, part, ring, mine, pieces, done,
    in_send, in_recv, pot_send, pot_recv, share_send, share_recv, col_send, col_recv,
    meet_send, meet_recv, core_send, core_recv, home_send, home_recv,
    ring_send, ring_recv, piece_send, piece_recv, out_send, out_recv, near_sem,
):
    me, band = lax.axis_index("space"), lax.axis_index("band")
    core, pair = lax.rem(band, 2), lax.div(band, 2)
    y, z_hi = lax.rem(pair, N_Y), lax.div(pair, N_Y)
    spot = z_hi * SPACE + me
    seat = 2 * y + core

    def wrap(value, size):
        return jnp.where(value >= size, value - size, value)

    def split(index):
        hi = jnp.where(index >= SPACE, 1, 0)
        return hi, index - SPACE * hi

    def arrival(target, semaphore):
        pltpu.make_async_copy(target, target, semaphore).wait()

    def band_of(hi, a_y):
        return (hi * N_Y + a_y) * 2 + core

    def spot_device(index):
        hi, rest = split(index)
        return (rest, band_of(hi, y))

    def seat_device(index):
        return (me, z_hi * 2 * N_Y + index)

    other = seat_device(2 * y + 1 - core)
    up = (me, band_of(z_hi, wrap(y + 1, N_Y)))
    down = (me, band_of(z_hi, wrap(y + N_Y - 1, N_Y)))

    def copy(source, target, send, recv, peer):
        return pltpu.make_async_remote_copy(
            src_ref=source, dst_ref=target, send_sem=send, recv_sem=recv,
            device_id=peer, device_id_type=MESH,
        )

    def each(low, high, body):
        def step(k, carry):
            body(k)
            return carry

        lax.fori_loop(low, high, step, 0)

    closers = []
    barrier = pltpu.get_barrier_semaphore()

    def greet(peer):
        pl.semaphore_signal(barrier, inc=1, device_id=peer, device_id_type=MESH)

    each(1, SPOTS, lambda k: greet(spot_device(wrap(spot + k, SPOTS))))
    each(1, 2 * N_Y, lambda k: greet(seat_device(wrap(seat + k, 2 * N_Y))))
    pl.semaphore_wait(barrier, SPOTS - 1 + 2 * N_Y - 1)

    def pot_copy(k, source):
        peer = wrap(me + k, SPACE)
        return copy(
            pot_ref.at[pl.ds(2 * seat, 2)], pot.at[source, pl.ds(2 * seat, 2)],
            pot_send.at[k], pot_recv.at[source], (peer, band),
        )

    def in_copy(k, source):
        peer = wrap(me + k, SPACE)
        return copy(
            orbs_ref.at[peer], field.at[1 + source],
            in_send.at[k], in_recv.at[source], (peer, band),
        )

    each(1, SPACE, lambda k: pot_copy(k, me).start())
    each(1, SPACE, lambda k: in_copy(k, me).start())
    closers.append(lambda: each(1, SPACE, lambda k: pot_copy(k, me).wait_send()))
    closers.append(lambda: each(1, SPACE, lambda k: in_copy(k, me).wait_send()))
    pltpu.make_async_copy(orbs_ref.at[me], field.at[1 + me], in_recv.at[me]).start()
    pltpu.make_async_copy(
        pot_ref.at[pl.ds(2 * seat, 2)], pot.at[me, pl.ds(2 * seat, 2)], pot_recv.at[me]
    ).start()
    each(0, SPACE, lambda j: arrival(pot.at[j, pl.ds(2 * seat, 2)], pot_recv.at[j]))

    def share(k, source):
        place = pot.at[:, pl.ds(2 * source, 2)]
        return copy(
            place, place, share_send.at[k], share_recv.at[source],
            seat_device(wrap(seat + k, 2 * N_Y)),
        )

    each(1, 2 * N_Y, lambda k: share(k, seat).start())
    closers.append(lambda: each(1, 2 * N_Y, lambda k: share(k, seat).wait_send()))
    each(0, SPACE, lambda j: arrival(field.at[1 + j], in_recv.at[j]))
    each(1, 2 * N_Y, lambda k: share(k, wrap(seat + k, 2 * N_Y)).wait_recv())

    shape = (2, 32, LANES)
    lane = lax.broadcasted_iota(jnp.int32, shape, 2)
    low_half = lane < NZ
    deep = lane & (NZ - 1)
    low_plane = (lax.broadcasted_iota(jnp.int32, shape, 1) & 1) == 0
    near_weight, far_weight = -1.0 / 6.0, 1.0 / 96.0

    def applied(source, at):
        center = source[pl.ds(at + 1, 2)]
        before = source[pl.ds(at, 2)]
        after = source[pl.ds(at + 2, 2)]
        swap = pltpu.roll(center, NZ, axis=2)
        pairs = (center + jnp.where(low_plane, after, before)).reshape(8, 8, LANES)
        near = jnp.where(
            low_plane,
            pltpu.roll(pairs, 7, axis=1).reshape(shape),
            pltpu.roll(pairs, 1, axis=1).reshape(shape),
        ) + swap
        near = near + pltpu.roll(jnp.where(deep == 0, swap, center), LANES - 1, axis=2)
        near = near + pltpu.roll(jnp.where(deep == NZ - 1, swap, center), 1, axis=2)
        far = before + after
        far = far + pltpu.roll(jnp.where(deep < 2, swap, center), LANES - 2, axis=2)
        far = far + pltpu.roll(jnp.where(deep >= NZ - 2, swap, center), 2, axis=2)
        beside = near_weight * swap
        both = far_weight * center
        shifted = pltpu.roll(jnp.where(low_half, beside + both, both), 2, axis=1)
        shifted = shifted + pltpu.roll(jnp.where(low_half, both, beside + both), 30, axis=1)
        level = (pot[pl.ds(at, 2)] - 2.25) * 0.25
        return level * center + near * near_weight + far * far_weight + shifted

    def wrapped(target):
        target[0] = target[SPACE]
        target[SPACE + 1] = target[1]

    def stage_1(i):
        first[pl.ds(2 * i + 1, 2)] = applied(field, 2 * i)

    def stage_2(i):
        second[pl.ds(2 * i + 1, 2)] = 2.0 * applied(first, 2 * i) - field[pl.ds(2 * i + 1, 2)]

    def col_copy(tile, hi, rest):
        return copy(
            last.at[rest, pl.ds(16 * hi + 8 * tile, 8)],
            column.at[spot, pl.ds(8 * tile, 8)],
            col_send.at[tile, SPACE * hi + rest], col_recv.at[tile, spot], (rest, band_of(hi, y)),
        )

    def start_col(tile, rest):
        for hi in range(2):
            @pl.when((rest != me) | (hi != z_hi))
            def _():
                col_copy(tile, hi, rest).start()

    def stage_3(i):
        j = wrap(begin + i, 12)
        last[pl.ds(2 * j, 2)] = 2.0 * applied(second, 2 * j) - first[pl.ds(2 * j + 1, 2)]
        for n in range(2):
            start_col(0, 2 * j + n)

    wrapped(field)
    each(0, 12, stage_1)
    wrapped(first)
    each(0, 12, stage_2)
    wrapped(second)
    begin = lax.div(me, 2)
    each(0, 12, stage_3)
    each(0, SPACE, lambda k: start_col(1, wrap(me + k, SPACE)))
    for tile in range(2):
        pltpu.make_async_copy(
            last.at[me, pl.ds(pl.multiple_of(16 * z_hi + 8 * tile, 8), 8)],
            column.at[spot, pl.ds(8 * tile, 8)], col_recv.at[tile, spot],
        ).start()

    def finish_col(rest):
        for tile in range(2):
            for hi in range(2):
                @pl.when((rest != me) | (hi != z_hi))
                def _():
                    col_copy(tile, hi, rest).wait_send()

    closers.append(lambda: each(0, SPACE, finish_col))

    def band_place(k, hi, a_y):
        return held.at[k, pl.ds(pl.multiple_of(ROWS * band_of(hi, a_y), 8), ROWS)]

    def meet_copy(k, hi, a_y, source):
        return copy(
            column.at[pl.ds(SPACE * hi, SPACE), 8 * (a_y & 1) + (a_y - (a_y & 1)) + k],
            band_place(k, hi, source),
            meet_send.at[hi, k, a_y], meet_recv.at[hi, k, source],
            (me, band_of(z_hi, a_y)),
        )

    def own_copy(k, hi):
        return pltpu.make_async_copy(
            column.at[pl.ds(SPACE * hi, SPACE), 8 * (y & 1) + (y - (y & 1)) + k],
            band_place(k, hi, y), meet_recv.at[hi, k, y],
        )

    for tile in range(2):
        each(0, SPOTS, lambda j: arrival(column.at[j, pl.ds(8 * tile, 8)], col_recv.at[tile, j]))

        def meet(i):
            a_y = ((y - (y & 1) + 2 * i) & 7) + tile

            @pl.when(a_y != y)
            def _():
                for hi in range(2):
                    for k in range(2):
                        meet_copy(k, hi, a_y, y).start()

            @pl.when(a_y == y)
            def _():
                for hi in range(2):
                    for k in range(2):
                        own_copy(k, hi).start()

        each(0, 4, meet)

    def finish_meet(i):
        for hi in range(2):
            for k in range(2):
                meet_copy(k, hi, (y + i) & 7, y).wait_send()

    closers.append(lambda: each(1, N_Y, finish_meet))

    def across(j, a_core):
        place = held.at[:, pl.ds(pl.multiple_of(ROWS * (2 * j + a_core), 8), ROWS)]
        return copy(place, place, core_send.at[j], core_recv.at[j], other)

    for hi in range(2):
        for k in range(2):
            own_copy(k, hi).wait()
        across(hi * N_Y + y, core).start()

    def arrived(i):
        source = (y + i) & 7
        for hi in range(2):
            for k in range(2):
                meet_copy(k, hi, source, source).wait_recv()
            across(hi * N_Y + source, core).start()

    each(1, N_Y, arrived)
    each(0, 2 * N_Y, lambda j: across(j, 1 - core).wait_recv())
    closers.append(lambda: each(0, 2 * N_Y, lambda j: across(j, core).wait_send()))

    near_rows = pl.multiple_of(16 * z_hi, 8)
    away = pl.multiple_of(16 - 16 * z_hi, 8)

    def home_copy(k, orbital):
        peer = wrap(me + k, SPACE)
        return copy(
            last.at[peer, pl.ds(away, 16)], home_ref.at[orbital, pl.ds(away, 16)],
            home_send.at[k], home_recv.at[orbital], (peer, band),
        )

    each(1, EARLY, lambda k: home_copy(k, me).start())
    near_copy = pltpu.make_async_copy(
        column.at[pl.ds(SPACE * z_hi, SPACE)], home_ref.at[:, pl.ds(near_rows, 16)], near_sem
    )
    near_copy.start()
    closers.append(near_copy.wait)
    pltpu.make_async_copy(
        last.at[me, pl.ds(away, 16)], home_ref.at[me, pl.ds(away, 16)], home_recv.at[me]
    ).start()

    for g in range(2 * N_Y):
        for k in range(2):
            rows[g, :, LANES * k:LANES * (k + 1)] = held[
                k, pl.ds(pl.multiple_of(ROWS * (2 * g + core), 8), ROWS), :
            ]
    left = rows[...].reshape(2 * N_Y * ROWS, 2 * LANES)
    left_hi = left.astype(jnp.bfloat16)
    left_lo = (left - left_hi.astype(jnp.float32)).astype(jnp.bfloat16)
    left_cat = jnp.concatenate([left_hi, left_hi, left_lo], axis=1)
    for k in range(2):
        cells = held[k]
        cells_hi = cells.astype(jnp.bfloat16)
        cells_lo = (cells - cells_hi.astype(jnp.float32)).astype(jnp.bfloat16)
        for slot, value in enumerate((cells_hi, cells_lo, cells_hi)):
            cat[:, 2 * LANES * slot + LANES * k:2 * LANES * slot + LANES * (k + 1)] = value
    for n in range(3):
        block = lax.dot_general(
            left_cat, cat[256 * n:256 * (n + 1), :], (((1,), (1,)), ((), ())),
            preferred_element_type=jnp.float32,
        )
        part[:, :, :, 256 * n:256 * (n + 1)] = block.reshape(2, N_Y, ROWS, 256)

    def hop(way, step, h, source):
        return copy(
            source, ring.at[way, step, h],
            ring_send.at[way, step, h], ring_recv.at[way, step, h], up if way == 0 else down,
        )

    def goal(way, step):
        return (y + (4 - step if way == 0 else 4 + step)) & 7

    for way in range(2):
        hop(way, 0, way, part.at[way, goal(way, 0)]).start()
    for way in range(2):
        hop(way, 1, 1 - way, part.at[1 - way, goal(way, 1)]).start()
    for step in range(4):
        for turn in range(2 if step else 1):
            for way in range(2):
                h = way if turn == 1 or step == 0 else 1 - way
                slot = ring.at[way, step, h]
                hop(way, step, h, slot).wait_recv()
                if step < 3:
                    ring[way, step, h] = ring[way, step, h] + part[h, goal(way, step + 1)]
                    hop(way, step + 1, h, slot).start()

    def finish_ring():
        for way in range(2):
            for step in range(4):
                for h in range(2):
                    if step > 0 or h == way:
                        hop(way, step, h, ring.at[way, step, h]).wait_send()

    closers.append(finish_ring)

    for h in range(2):
        total = part[h, y] + ring[0, 3, h] + ring[1, 3, h]
        for t in range(TILES):
            mine[ROWS * h:ROWS * (h + 1), t, :] = total[:, LANES * t:LANES * (t + 1)]

    def piece(k, source):
        peer = wrap(spot + k, SPOTS)
        return copy(
            mine.at[peer], pieces.at[source],
            piece_send.at[k], piece_recv.at[source], spot_device(peer),
        )

    each(1, SPOTS, lambda k: piece(k, spot).start())
    pltpu.make_async_copy(mine.at[spot], pieces.at[spot], piece_recv.at[spot]).start()
    each(0, SPOTS, lambda j: arrival(pieces.at[j], piece_recv.at[j]))
    closers.append(lambda: each(1, SPOTS, lambda k: piece(k, spot).wait_send()))
    done[me] = jnp.sum(pieces[...], axis=0) * (1.0 / CELLS)

    def give(k, source):
        peer = wrap(me + k, SPACE)
        return copy(
            done.at[me], done.at[source], out_send.at[k], out_recv.at[source], (peer, band)
        )

    each(1, SPACE, lambda k: give(k, me).start())
    each(EARLY, SPACE, lambda k: home_copy(k, me).start())
    closers.append(lambda: each(0, SPACE, lambda j: arrival(home_ref.at[j, pl.ds(away, 16)], home_recv.at[j])))
    closers.append(lambda: each(1, SPACE, lambda k: home_copy(k, me).wait_send()))
    each(1, SPACE, lambda k: give(k, wrap(me + k, SPACE)).wait_recv())
    closers.append(lambda: each(1, SPACE, lambda k: give(k, me).wait_send()))
    for t in range(TILES):
        margin_ref[:, LANES * t:LANES * (t + 1)] = done[:, t, :]

    for closer in closers:
        closer()


def shards(orbitals, potential):
    dma = pltpu.SemaphoreType.DMA
    f32 = jnp.float32
    vmem = pl.BlockSpec(memory_space=pltpu.VMEM)
    stay = pl.BlockSpec(memory_space=pl.ANY)
    padded = pltpu.VMEM((SPACE + 2, 32, LANES), f32)
    home, margin = pl.pallas_call(
        kernel,
        out_shape=(
            jax.ShapeDtypeStruct((ROWS, 32, LANES), f32),
            jax.ShapeDtypeStruct((ROWS, ORBS), f32),
        ),
        in_specs=[pl.BlockSpec(memory_space=pltpu.HBM)] * 2,
        out_specs=(stay, vmem),
        scratch_shapes=[
            padded, padded, padded,
            pltpu.VMEM((SPACE, 32, LANES), f32),
            pltpu.VMEM((SPACE, 32, LANES), f32),
            pltpu.VMEM((SPOTS, 16, LANES), f32),
            pltpu.VMEM((2, ORBS, LANES), f32),
            pltpu.VMEM((2 * N_Y, ROWS, 2 * LANES), f32),
            pltpu.VMEM((ORBS, 6 * LANES), jnp.bfloat16),
            pltpu.VMEM((2, N_Y, ROWS, ORBS), f32),
            pltpu.VMEM((2, 4, 2, ROWS, ORBS), f32),
            pltpu.VMEM((SPOTS, TILES, LANES), f32),
            pltpu.VMEM((SPOTS, TILES, LANES), f32),
            pltpu.VMEM((ROWS, TILES, LANES), f32),
            dma((SPACE,)), dma((SPACE,)), dma((SPACE,)), dma((SPACE,)),
            dma((2 * N_Y,)), dma((2 * N_Y,)), dma((2, SPOTS)), dma((2, SPOTS)),
            dma((2, 2, N_Y)), dma((2, 2, N_Y)), dma((2 * N_Y,)), dma((2 * N_Y,)),
            dma((SPACE,)), dma((SPACE,)),
            dma((2, 4, 2)), dma((2, 4, 2)), dma((SPOTS,)), dma((SPOTS,)), dma((SPACE,)), dma((SPACE,)), dma,
        ],
        compiler_params=pltpu.CompilerParams(
            collective_id=0, has_side_effects=True, vmem_limit_bytes=20 << 20
        ),
    )(
        orbitals.reshape(ROWS, 2, 16, LANES).transpose(0, 2, 1, 3).reshape(ROWS, 32, LANES),
        potential.reshape(2, 16, LANES).transpose(1, 0, 2).reshape(32, LANES),
    )
    filtered = home.reshape(ROWS, 16, 2, LANES).transpose(0, 2, 1, 3).reshape(ROWS, 2, 2048)
    return (filtered, margin)


def solution(mesh):
    return jax.shard_map(
        shards,
        mesh=mesh,
        in_specs=(P("band", "space", None), P("space", None)),
        out_specs=(P("band", "space", None), P("band", None)),
        check_vma=False,
    )
```

```python
import jax
import jax.numpy as jnp
from jax import lax
from jax.experimental import pallas as pl
from jax.experimental.pallas import tpu as pltpu
from jax.sharding import PartitionSpec as P

MESH = pl.DeviceIdType.MESH
NZ_LO, N_Y = 6, 8
SPACE = 24
SPOTS = 2 * SPACE
NZ = 64
ROWS = 24
ORBS = 768
LANES = 128
TILES = ORBS // LANES
CELLS = 48 * 2048


def kernel(
    orbs_ref, pot_ref, home_ref, margin_ref,
    field, first, second, last, pot, column, held, rows, cat, part, ring, mine, pieces, done,
    in_send, in_recv, pot_send, pot_recv, share_send, share_recv, col_send, col_recv,
    meet_send, meet_recv, core_send, core_recv, home_send, home_recv,
    ring_send, ring_recv, piece_send, piece_recv, out_send, out_recv, near_sem,
):
    me, band = lax.axis_index("space"), lax.axis_index("band")
    core, pair = lax.rem(band, 2), lax.div(band, 2)
    y, z_hi = lax.rem(pair, N_Y), lax.div(pair, N_Y)
    spot = z_hi * SPACE + me
    seat = 2 * y + core

    def wrap(value, size):
        return jnp.where(value >= size, value - size, value)

    def split(index):
        hi = jnp.where(index >= SPACE, 1, 0)
        return hi, index - SPACE * hi

    def arrival(target, semaphore):
        pltpu.make_async_copy(target, target, semaphore).wait()

    def band_of(hi, a_y):
        return (hi * N_Y + a_y) * 2 + core

    def spot_device(index):
        hi, rest = split(index)
        return (rest, band_of(hi, y))

    def seat_device(index):
        return (me, z_hi * 2 * N_Y + index)

    other = seat_device(2 * y + 1 - core)
    up = (me, band_of(z_hi, wrap(y + 1, N_Y)))
    down = (me, band_of(z_hi, wrap(y + N_Y - 1, N_Y)))

    def copy(source, target, send, recv, peer):
        return pltpu.make_async_remote_copy(
            src_ref=source, dst_ref=target, send_sem=send, recv_sem=recv,
            device_id=peer, device_id_type=MESH,
        )

    def each(low, high, body):
        def step(k, carry):
            body(k)
            return carry

        lax.fori_loop(low, high, step, 0)

    closers = []
    barrier = pltpu.get_barrier_semaphore()

    def greet(peer):
        pl.semaphore_signal(barrier, inc=1, device_id=peer, device_id_type=MESH)

    each(12, SPOTS, lambda k: greet(spot_device(wrap(spot + k, SPOTS))))
    each(1, 12, lambda k: greet(spot_device(wrap(spot + k, SPOTS))))
    each(1, 2 * N_Y, lambda k: greet(seat_device(wrap(seat + k, 2 * N_Y))))
    pl.semaphore_wait(barrier, SPOTS - 1 + 2 * N_Y - 1)

    def pot_copy(k, source):
        peer = wrap(me + k, SPACE)
        return copy(
            pot_ref.at[pl.ds(2 * seat, 2)], pot.at[source, pl.ds(2 * seat, 2)],
            pot_send.at[k], pot_recv.at[source], (peer, band),
        )

    def in_copy(k, source):
        peer = wrap(me + k, SPACE)
        return copy(
            orbs_ref.at[peer], field.at[1 + source],
            in_send.at[k], in_recv.at[source], (peer, band),
        )

    each(1, SPACE, lambda k: pot_copy(k, me).start())
    each(1, SPACE, lambda k: in_copy(k, me).start())
    closers.append(lambda: each(1, SPACE, lambda k: pot_copy(k, me).wait_send()))
    closers.append(lambda: each(1, SPACE, lambda k: in_copy(k, me).wait_send()))
    pltpu.make_async_copy(orbs_ref.at[me], field.at[1 + me], in_recv.at[me]).start()
    pltpu.make_async_copy(
        pot_ref.at[pl.ds(2 * seat, 2)], pot.at[me, pl.ds(2 * seat, 2)], pot_recv.at[me]
    ).start()
    each(0, SPACE, lambda j: arrival(pot.at[j, pl.ds(2 * seat, 2)], pot_recv.at[j]))

    def share(k, source):
        place = pot.at[:, pl.ds(2 * source, 2)]
        return copy(
            place, place, share_send.at[k], share_recv.at[source],
            seat_device(wrap(seat + k, 2 * N_Y)),
        )

    each(1, 2 * N_Y, lambda k: share(k, seat).start())
    closers.append(lambda: each(1, 2 * N_Y, lambda k: share(k, seat).wait_send()))
    each(0, SPACE, lambda j: arrival(field.at[1 + j], in_recv.at[j]))
    each(1, 2 * N_Y, lambda k: share(k, wrap(seat + k, 2 * N_Y)).wait_recv())

    shape = (2, 32, LANES)
    lane = lax.broadcasted_iota(jnp.int32, shape, 2)
    low_half = lane < NZ
    deep = lane & (NZ - 1)
    low_plane = (lax.broadcasted_iota(jnp.int32, shape, 1) & 1) == 0
    near_weight, far_weight = -1.0 / 6.0, 1.0 / 96.0

    def applied(source, at):
        center = source[pl.ds(at + 1, 2)]
        before = source[pl.ds(at, 2)]
        after = source[pl.ds(at + 2, 2)]
        swap = pltpu.roll(center, NZ, axis=2)
        pairs = (center + jnp.where(low_plane, after, before)).reshape(8, 8, LANES)
        near = jnp.where(
            low_plane,
            pltpu.roll(pairs, 7, axis=1).reshape(shape),
            pltpu.roll(pairs, 1, axis=1).reshape(shape),
        ) + swap
        near = near + pltpu.roll(jnp.where(deep == 0, swap, center), LANES - 1, axis=2)
        near = near + pltpu.roll(jnp.where(deep == NZ - 1, swap, center), 1, axis=2)
        far = before + after
        far = far + pltpu.roll(jnp.where(deep < 2, swap, center), LANES - 2, axis=2)
        far = far + pltpu.roll(jnp.where(deep >= NZ - 2, swap, center), 2, axis=2)
        beside = near_weight * swap
        both = far_weight * center
        shifted = pltpu.roll(jnp.where(low_half, beside + both, both), 2, axis=1)
        shifted = shifted + pltpu.roll(jnp.where(low_half, both, beside + both), 30, axis=1)
        level = (pot[pl.ds(at, 2)] - 2.25) * 0.25
        return level * center + near * near_weight + far * far_weight + shifted

    def wrapped(target):
        target[0] = target[SPACE]
        target[SPACE + 1] = target[1]

    def stage_1(i):
        first[pl.ds(2 * i + 1, 2)] = applied(field, 2 * i)

    def stage_2(i):
        second[pl.ds(2 * i + 1, 2)] = 2.0 * applied(first, 2 * i) - field[pl.ds(2 * i + 1, 2)]

    def col_copy(tile, hi, rest):
        return copy(
            last.at[rest, pl.ds(16 * hi + 8 * tile, 8)],
            column.at[spot, pl.ds(8 * tile, 8)],
            col_send.at[tile, SPACE * hi + rest], col_recv.at[tile, spot], (rest, band_of(hi, y)),
        )

    def start_col(tile, rest):
        for hi in range(2):
            @pl.when((rest != me) | (hi != z_hi))
            def _():
                col_copy(tile, hi, rest).start()

    def stage_3(i):
        j = wrap(begin + i, 12)
        last[pl.ds(2 * j, 2)] = 2.0 * applied(second, 2 * j) - first[pl.ds(2 * j + 1, 2)]
        for n in range(2):
            start_col(0, 2 * j + n)

    wrapped(field)
    each(0, 12, stage_1)
    wrapped(first)
    each(0, 12, stage_2)
    wrapped(second)
    begin = lax.div(me, 2)
    each(0, 12, stage_3)
    each(0, SPACE, lambda k: start_col(1, wrap(me + k, SPACE)))
    for tile in range(2):
        pltpu.make_async_copy(
            last.at[me, pl.ds(pl.multiple_of(16 * z_hi + 8 * tile, 8), 8)],
            column.at[spot, pl.ds(8 * tile, 8)], col_recv.at[tile, spot],
        ).start()

    def finish_col(rest):
        for tile in range(2):
            for hi in range(2):
                @pl.when((rest != me) | (hi != z_hi))
                def _():
                    col_copy(tile, hi, rest).wait_send()

    closers.append(lambda: each(0, SPACE, finish_col))

    def band_place(k, hi, a_y):
        return held.at[k, pl.ds(pl.multiple_of(ROWS * band_of(hi, a_y), 8), ROWS)]

    def meet_copy(k, hi, a_y, source):
        return copy(
            column.at[pl.ds(SPACE * hi, SPACE), 8 * (a_y & 1) + (a_y - (a_y & 1)) + k],
            band_place(k, hi, source),
            meet_send.at[hi, k, a_y], meet_recv.at[hi, k, source],
            (me, band_of(z_hi, a_y)),
        )

    def own_copy(k, hi):
        return pltpu.make_async_copy(
            column.at[pl.ds(SPACE * hi, SPACE), 8 * (y & 1) + (y - (y & 1)) + k],
            band_place(k, hi, y), meet_recv.at[hi, k, y],
        )

    for tile in range(2):
        each(0, SPOTS, lambda j: arrival(column.at[j, pl.ds(8 * tile, 8)], col_recv.at[tile, j]))

        def meet(i):
            a_y = ((y - (y & 1) + 2 * i) & 7) + tile

            @pl.when(a_y != y)
            def _():
                for hi in range(2):
                    for k in range(2):
                        meet_copy(k, hi, a_y, y).start()

            @pl.when(a_y == y)
            def _():
                for hi in range(2):
                    for k in range(2):
                        own_copy(k, hi).start()

        each(0, 4, meet)

    def finish_meet(i):
        for hi in range(2):
            for k in range(2):
                meet_copy(k, hi, (y + i) & 7, y).wait_send()

    closers.append(lambda: each(1, N_Y, finish_meet))

    def across(j, a_core):
        place = held.at[:, pl.ds(pl.multiple_of(ROWS * (2 * j + a_core), 8), ROWS)]
        return copy(place, place, core_send.at[j], core_recv.at[j], other)

    for hi in range(2):
        for k in range(2):
            own_copy(k, hi).wait()
        across(hi * N_Y + y, core).start()

    def arrived(i):
        source = (y + i) & 7
        for hi in range(2):
            for k in range(2):
                meet_copy(k, hi, source, source).wait_recv()
            across(hi * N_Y + source, core).start()

    each(1, N_Y, arrived)
    each(0, 2 * N_Y, lambda j: across(j, 1 - core).wait_recv())
    closers.append(lambda: each(0, 2 * N_Y, lambda j: across(j, core).wait_send()))

    near_rows = pl.multiple_of(16 * z_hi, 8)
    away = pl.multiple_of(16 - 16 * z_hi, 8)

    def home_copy(k, orbital):
        peer = wrap(me + k, SPACE)
        return copy(
            last.at[peer, pl.ds(away, 16)], home_ref.at[orbital, pl.ds(away, 16)],
            home_send.at[k], home_recv.at[orbital], (peer, band),
        )

    homeward = iter(range(1, SPACE))
    near_copy = pltpu.make_async_copy(
        column.at[pl.ds(SPACE * z_hi, SPACE)], home_ref.at[:, pl.ds(near_rows, 16)], near_sem
    )
    near_copy.start()
    closers.append(near_copy.wait)
    pltpu.make_async_copy(
        last.at[me, pl.ds(away, 16)], home_ref.at[me, pl.ds(away, 16)], home_recv.at[me]
    ).start()

    def hop(way, step, h, source):
        return copy(
            source, ring.at[way, step, h],
            ring_send.at[way, step, h], ring_recv.at[way, step, h], up if way == 0 else down,
        )

    def goal(way, step):
        return (4 - step if way == 0 else 4 + step) % N_Y

    for k in range(2):
        cells = held[k]
        cells_hi = cells.astype(jnp.bfloat16)
        cells_lo = (cells - cells_hi.astype(jnp.float32)).astype(jnp.bfloat16)
        for slot, value in enumerate((cells_hi, cells_lo, cells_hi)):
            cat[:, 2 * LANES * slot + LANES * k:2 * LANES * slot + LANES * (k + 1)] = value
    for away_by in ((4, 3, 5), (2, 6, 1, 7, 0)):
        groups = [(offset, h) for offset in away_by for h in range(2)]
        for g, (offset, h) in enumerate(groups):
            owner = 2 * (N_Y * h + ((y + offset) & 7)) + core
            for k in range(2):
                rows[g, :, LANES * k:LANES * (k + 1)] = held[
                    k, pl.ds(pl.multiple_of(ROWS * owner, 8), ROWS), :
                ]
        left = rows[0:len(groups)].reshape(len(groups) * ROWS, 2 * LANES)
        left_hi = left.astype(jnp.bfloat16)
        left_lo = (left - left_hi.astype(jnp.float32)).astype(jnp.bfloat16)
        left_cat = jnp.concatenate([left_hi, left_hi, left_lo], axis=1)
        for n in range(3):
            block = lax.dot_general(
                left_cat, cat[256 * n:256 * (n + 1), :], (((1,), (1,)), ((), ())),
                preferred_element_type=jnp.float32,
            ).reshape(len(groups), ROWS, 256)
            for g, (offset, h) in enumerate(groups):
                part[h, offset, :, 256 * n:256 * (n + 1)] = block[g]
        if 4 in away_by:
            for way in range(2):
                hop(way, 0, way, part.at[way, goal(way, 0)]).start()
            for way in range(2):
                hop(way, 1, 1 - way, part.at[1 - way, goal(way, 1)]).start()
            for _ in range(3):
                home_copy(next(homeward), me).start()

    for step in range(4):
        for turn in range(2 if step else 1):
            for way in range(2):
                h = way if turn == 1 or step == 0 else 1 - way
                slot = ring.at[way, step, h]
                hop(way, step, h, slot).wait_recv()
                if step < 3:
                    ring[way, step, h] = ring[way, step, h] + part[h, goal(way, step + 1)]
                    hop(way, step + 1, h, slot).start()
                    for _ in range(2):
                        home_copy(next(homeward), me).start()

    assert next(homeward, None) is None

    def finish_ring():
        for way in range(2):
            for step in range(4):
                for h in range(2):
                    if step > 0 or h == way:
                        hop(way, step, h, ring.at[way, step, h]).wait_send()

    closers.append(finish_ring)

    for h in range(2):
        total = part[h, 0] + ring[0, 3, h] + ring[1, 3, h]
        for t in range(TILES):
            mine[ROWS * h:ROWS * (h + 1), t, :] = total[:, LANES * t:LANES * (t + 1)]

    def piece(k, source):
        peer = wrap(spot + k, SPOTS)
        return copy(
            mine.at[peer], pieces.at[source],
            piece_send.at[k], piece_recv.at[source], spot_device(peer),
        )

    each(1, SPOTS, lambda k: piece(k, spot).start())
    pltpu.make_async_copy(mine.at[spot], pieces.at[spot], piece_recv.at[spot]).start()
    each(0, SPOTS, lambda j: arrival(pieces.at[j], piece_recv.at[j]))
    closers.append(lambda: each(1, SPOTS, lambda k: piece(k, spot).wait_send()))
    done[me] = jnp.sum(pieces[...], axis=0) * (1.0 / CELLS)

    def give(k, source):
        peer = wrap(me + k, SPACE)
        return copy(
            done.at[me], done.at[source], out_send.at[k], out_recv.at[source], (peer, band)
        )

    each(1, SPACE, lambda k: give(k, me).start())
    closers.append(lambda: each(0, SPACE, lambda j: arrival(home_ref.at[j, pl.ds(away, 16)], home_recv.at[j])))
    closers.append(lambda: each(1, SPACE, lambda k: home_copy(k, me).wait_send()))
    each(1, SPACE, lambda k: give(k, wrap(me + k, SPACE)).wait_recv())
    closers.append(lambda: each(1, SPACE, lambda k: give(k, me).wait_send()))
    for t in range(TILES):
        margin_ref[:, LANES * t:LANES * (t + 1)] = done[:, t, :]

    for closer in closers:
        closer()


def shards(orbitals, potential):
    dma = pltpu.SemaphoreType.DMA
    f32 = jnp.float32
    vmem = pl.BlockSpec(memory_space=pltpu.VMEM)
    stay = pl.BlockSpec(memory_space=pl.ANY)
    padded = pltpu.VMEM((SPACE + 2, 32, LANES), f32)
    home, margin = pl.pallas_call(
        kernel,
        out_shape=(
            jax.ShapeDtypeStruct((ROWS, 32, LANES), f32),
            jax.ShapeDtypeStruct((ROWS, ORBS), f32),
        ),
        in_specs=[pl.BlockSpec(memory_space=pltpu.HBM)] * 2,
        out_specs=(stay, vmem),
        scratch_shapes=[
            padded, padded, padded,
            pltpu.VMEM((SPACE, 32, LANES), f32),
            pltpu.VMEM((SPACE, 32, LANES), f32),
            pltpu.VMEM((SPOTS, 16, LANES), f32),
            pltpu.VMEM((2, ORBS, LANES), f32),
            pltpu.VMEM((10, ROWS, 2 * LANES), f32),
            pltpu.VMEM((ORBS, 6 * LANES), jnp.bfloat16),
            pltpu.VMEM((2, N_Y, ROWS, ORBS), f32),
            pltpu.VMEM((2, 4, 2, ROWS, ORBS), f32),
            pltpu.VMEM((SPOTS, TILES, LANES), f32),
            pltpu.VMEM((SPOTS, TILES, LANES), f32),
            pltpu.VMEM((ROWS, TILES, LANES), f32),
            dma((SPACE,)), dma((SPACE,)), dma((SPACE,)), dma((SPACE,)),
            dma((2 * N_Y,)), dma((2 * N_Y,)), dma((2, SPOTS)), dma((2, SPOTS)),
            dma((2, 2, N_Y)), dma((2, 2, N_Y)), dma((2 * N_Y,)), dma((2 * N_Y,)),
            dma((SPACE,)), dma((SPACE,)),
            dma((2, 4, 2)), dma((2, 4, 2)), dma((SPOTS,)), dma((SPOTS,)), dma((SPACE,)), dma((SPACE,)), dma,
        ],
        compiler_params=pltpu.CompilerParams(
            collective_id=0, has_side_effects=True, vmem_limit_bytes=20 << 20
        ),
    )(
        orbitals.reshape(ROWS, 2, 16, LANES).transpose(0, 2, 1, 3).reshape(ROWS, 32, LANES),
        potential.reshape(2, 16, LANES).transpose(1, 0, 2).reshape(32, LANES),
    )
    filtered = home.reshape(ROWS, 16, 2, LANES).transpose(0, 2, 1, 3).reshape(ROWS, 2, 2048)
    return (filtered, margin)


def solution(mesh):
    return jax.shard_map(
        shards,
        mesh=mesh,
        in_specs=(P("band", "space", None), P("space", None)),
        out_specs=(P("band", "space", None), P("band", None)),
        check_vma=False,
    )
```
